512 devices in a mesh: row: 16 (over z_hi, y), col: 32 (over z_lo, x, core).
Axes of the slice: x: 4, y: 4, z: 16 (z_hi: 4, z_lo: 4; z = z_hi * 4 + z_lo), core: 2. Of those that a mesh axis runs over, the one named last changes fastest.
Arguments:
- pair_state: bfloat16 [1536, 1536, 128], P('row', 'col'), may hold values from -6 to 6
- single_state: bfloat16 [1536, 384], P(('row', 'col')), may hold values from -6 to 6
- token_mask: int32 [1536], P('col'), may hold values 0 or 1
- first_gate: bfloat16 [128, 512], replicated, may hold values from -0.5 to 0.5
- first_up: bfloat16 [128, 512], replicated, may hold values from -0.5 to 0.5
- first_down: bfloat16 [512, 128], replicated, may hold values from -0.25 to 0.25
- bias_weight: bfloat16 [128, 16], replicated, may hold values from -21 to 21
- query_weight: bfloat16 [384, 384], replicated, may hold values from -0.3125 to 0.3125
- key_weight: bfloat16 [384, 384], replicated, may hold values from -0.3125 to 0.3125
- value_weight: bfloat16 [384, 384], replicated, may hold values from -0.3125 to 0.3125
- gate_weight: bfloat16 [384, 384], replicated, may hold values from -0.3125 to 0.3125
- out_weight: bfloat16 [384, 384], replicated, may hold values from -0.3125 to 0.3125
- second_gate: bfloat16 [128, 512], replicated, may hold values from -0.5 to 0.5
- second_up: bfloat16 [128, 512], replicated, may hold values from -0.5 to 0.5
- second_down: bfloat16 [512, 128], replicated, may hold values from -0.25 to 0.25
Outputs:
- pair_out: bfloat16 [1536, 1536, 128], P('row', 'col')
- single_out: bfloat16 [1536, 384], P('row')
The draws below stay inside these ranges and needn't reach their ends.
All inputs are finite; a program needn't handle non-finite values. No bound on the sum of `token_mask` on one device may be relied on, other than what follows from the above.
Results may differ from the reference program's by a relative error of at most 0.011.
Values may be sent and summed in bfloat16 or wider, within the bound.
No kernel may reach another device: no remote copies, remote signals or barrier semaphores. Data moves between devices by JAX's collectives and lax.ppermute only.
A program may use at most 64 MiB of HBM per device.

```python
import math
import jax
import jax.numpy as jnp
from jax import lax

C = 128
HID = 512
S = 384
HEADS = 16
HEAD_DIM = 24
N = 1536


def draw_bias_weight(key, part):
    first_key = jax.random.fold_in(key, 11)
    second_key = jax.random.fold_in(key, 12)
    entries = jax.random.normal(first_key, (C, HEADS), jnp.float32)
    scales = jnp.exp(jax.random.uniform(second_key, (HEADS,), jnp.float32, math.log(0.5), math.log(3.0)))
    return jnp.clip(entries * scales[None, :] / math.sqrt(C), -21.0, 21.0).astype(jnp.bfloat16)


def place_ends(values, stream_key, low, high):
    longest = values.shape.index(max(values.shape))
    spots = []
    for shift in (0, 1):
        where = [jax.random.randint(jax.random.fold_in(stream_key, axis), (), 0, length) for axis, length in enumerate(values.shape)]
        where[longest] = (where[longest] + shift) % values.shape[longest]
        spots.append(tuple(where))
    return values.at[spots[0]].set(low).at[spots[1]].set(high)


def level_of(stream_key, shape, shards, least, top_value):
    factor_of, own = 1.0, jax.random.fold_in(stream_key, 6)
    for position, blocks in shards:
        heights = jnp.exp(jax.random.uniform(jax.random.fold_in(own, position), (blocks,), jnp.float32, least / len(shards), top_value / len(shards)))
        factor_of = factor_of * jnp.repeat(heights, shape[position] // blocks).reshape([-1 if axis == position else 1 for axis in range(len(shape))])
    return factor_of


def scatter_about(key, dims, deviation, most, split=(), held_as=jnp.bfloat16):
    factor_of = level_of(key, dims, split, -0.22, 0.18) if split else 1.0
    drawn = jax.random.normal(key, dims, jnp.float32) * deviation * factor_of
    return jnp.minimum(jnp.maximum(drawn, -most), most).astype(held_as)


def setup_inputs(seed: int = 0) -> dict:
    streams_of = jax.random.split(jax.random.key(seed), 16)
    return {
        "pair_state": scatter_about(streams_of[0], (N, N, C), 1.0, 6.0, ((0, 16), (1, 32))),
        "single_state": scatter_about(streams_of[1], (N, S), 1.0, 6.0, ((0, 512),)),
        "token_mask": place_ends((jax.random.randint(streams_of[2], (N,), 0, 4) < 3).astype(jnp.int32), jax.random.fold_in(streams_of[2], 1), 0, 1),
        "first_gate": scatter_about(streams_of[3], (C, HID), C ** -0.5, 0.5),
        "first_up": scatter_about(streams_of[4], (C, HID), C ** -0.5, 0.5),
        "first_down": scatter_about(streams_of[5], (HID, C), HID ** -0.5, 0.25),
        "bias_weight": draw_bias_weight(jax.random.fold_in(streams_of[15], 71), 0),
        "query_weight": scatter_about(streams_of[7], (S, S), S ** -0.5, 0.3125),
        "key_weight": scatter_about(streams_of[8], (S, S), S ** -0.5, 0.3125),
        "value_weight": scatter_about(streams_of[9], (S, S), S ** -0.5, 0.3125),
        "gate_weight": scatter_about(streams_of[10], (S, S), S ** -0.5, 0.3125),
        "out_weight": scatter_about(streams_of[11], (S, S), S ** -0.5, 0.3125),
        "second_gate": scatter_about(streams_of[12], (C, HID), C ** -0.5, 0.5),
        "second_up": scatter_about(streams_of[13], (C, HID), C ** -0.5, 0.5),
        "second_down": scatter_about(streams_of[14], (HID, C), HID ** -0.5, 0.25),
    }


def norm_rows(values):
    centre = lax.optimization_barrier(jnp.mean(values, axis=-1, keepdims=True))
    centred = values - centre
    spread = lax.optimization_barrier(jnp.mean(centred * centred, axis=-1, keepdims=True))
    return centred * lax.rsqrt(spread + 1e-05)

def transition(widened, w_gate, w_up, w_down):
    layout = widened.shape
    flat_cells = widened.reshape(-1, layout[-1])
    normed = norm_rows(flat_cells).astype(jnp.bfloat16)
    gate_act = jnp.dot(normed, w_gate, preferred_element_type=jnp.float32)
    up_act = jnp.dot(normed, w_up, preferred_element_type=jnp.float32)
    hidden = (jax.nn.silu(gate_act) * up_act).astype(jnp.bfloat16)
    return jnp.dot(hidden, w_down, preferred_element_type=jnp.float32).reshape(layout)

def reference(pair_state, single_state, token_mask, first_gate, first_up, first_down, bias_weight, query_weight, key_weight, value_weight, gate_weight, out_weight, second_gate, second_up, second_down):
    blocks = N // 32
    stacked = pair_state.reshape(blocks, 32, N, C)

    def first_pass(pair_block):
        widened = pair_block.astype(jnp.float32)
        updated = (widened + transition(widened, first_gate, first_up, first_down)).astype(jnp.bfloat16)
        normed = norm_rows(updated.astype(jnp.float32)).astype(jnp.bfloat16)
        pair_bias = jnp.einsum('ijc,ch->ijh', normed.astype(jnp.float32), bias_weight.astype(jnp.float32), precision=lax.Precision.HIGHEST)
        return (updated, pair_bias)
    updated, pair_bias = lax.map(first_pass, stacked)
    updated = updated.reshape(N, N, C)
    pair_bias = jnp.transpose(pair_bias.reshape(N, N, HEADS), (2, 0, 1))
    flipped = jnp.transpose(updated, (1, 0, 2))

    def second_pass(halves):
        summed = halves[0].astype(jnp.float32) + halves[1].astype(jnp.float32)
        return (summed + transition(summed, second_gate, second_up, second_down)).astype(jnp.bfloat16)
    pair_out = lax.map(second_pass, (updated.reshape(blocks, 32, N, C), flipped.reshape(blocks, 32, N, C))).reshape(N, N, C)
    single_normed = norm_rows(single_state.astype(jnp.float32)).astype(jnp.bfloat16)
    queries = jnp.dot(single_normed, query_weight, preferred_element_type=jnp.float32).astype(jnp.bfloat16)
    key_vecs = jnp.dot(single_normed, key_weight, preferred_element_type=jnp.float32).astype(jnp.bfloat16)
    value_vecs = jnp.dot(single_normed, value_weight, preferred_element_type=jnp.float32).astype(jnp.bfloat16)
    gate_act = jax.nn.sigmoid(jnp.dot(single_normed, gate_weight, preferred_element_type=jnp.float32))
    query_heads = queries.astype(jnp.float32).reshape(N, HEADS, HEAD_DIM)
    key_heads = key_vecs.astype(jnp.float32).reshape(N, HEADS, HEAD_DIM)
    value_heads = value_vecs.astype(jnp.float32).reshape(N, HEADS, HEAD_DIM)
    scores = jnp.einsum('ihd,jhd->hij', query_heads, key_heads, precision=lax.Precision.HIGHEST) * (1.0 / math.sqrt(HEAD_DIM)) + pair_bias
    scores = jnp.where(token_mask[None, None, :] > 0, scores, -1000000000.0)
    row_top = lax.optimization_barrier(jnp.max(scores, axis=2, keepdims=True))
    weights = jnp.exp(scores - row_top)
    numerator = jnp.einsum('hij,jhd->ihd', weights, value_heads, precision=lax.Precision.HIGHEST)
    denominator = jnp.transpose(lax.optimization_barrier(jnp.sum(weights, axis=2)), (1, 0))
    attended = (numerator / denominator[:, :, None]).reshape(N, S)
    gated = (gate_act * attended).astype(jnp.bfloat16)
    single_out = (single_state.astype(jnp.float32) + jnp.dot(gated, out_weight, preferred_element_type=jnp.float32)).astype(jnp.bfloat16)
    return (pair_out, single_out)
```

```python
import math

import jax
import jax.numpy as jnp
from jax import lax
from jax.sharding import PartitionSpec as P

PAIR = ("row", "col")


def norm_rows(values):
    centre = jnp.mean(values, axis=-1, keepdims=True)
    centred = values - centre
    spread = jnp.mean(centred * centred, axis=-1, keepdims=True)
    return centred * lax.rsqrt(spread + 1e-05)


def transition(widened, w_gate, w_up, w_down):
    layout = widened.shape
    flat_cells = widened.reshape(-1, layout[-1])
    normed = norm_rows(flat_cells).astype(jnp.bfloat16)
    gate_act = jnp.dot(normed, w_gate, preferred_element_type=jnp.float32)
    up_act = jnp.dot(normed, w_up, preferred_element_type=jnp.float32)
    hidden = (jax.nn.silu(gate_act) * up_act).astype(jnp.bfloat16)
    return jnp.dot(hidden, w_down, preferred_element_type=jnp.float32).reshape(layout)


def mirror_pairs(flip):
    rows, cols = lax.axis_size("row"), lax.axis_size("col")
    pairs = []
    for row in range(rows):
        for col in range(cols):
            core, chip = col % 2, col // 2
            pairs.append((row * cols + col, chip * cols + 2 * row + (core ^ flip)))
    return pairs


def mirror(pair_block):
    half = pair_block.shape[0] // 2
    core = lax.axis_index("col") % 2
    same = lax.ppermute(
        lax.dynamic_slice_in_dim(pair_block, core * half, half, 0), PAIR, mirror_pairs(0)
    )
    other = lax.ppermute(
        lax.dynamic_slice_in_dim(pair_block, (1 - core) * half, half, 0), PAIR, mirror_pairs(1)
    )
    first = jnp.where(core == 0, same, other)
    second = jnp.where(core == 0, other, same)
    return jnp.concatenate(
        [jnp.transpose(first, (1, 0, 2)), jnp.transpose(second, (1, 0, 2))], axis=0
    )


def spread_rows(rows):
    count, channels = rows.shape
    cols = lax.axis_size("col")
    folded = rows.reshape(count * channels // 128, 128)
    padded = jnp.pad(folded, ((0, 16 - folded.shape[0]), (0, 0)))
    copies = jnp.broadcast_to(padded[None], (cols, 16, 128))
    got = lax.all_to_all(copies, "col", split_axis=0, concat_axis=0, tiled=True)
    return got[:, : folded.shape[0]].reshape(cols * count, channels)


def body(
    pair_state,
    single_state,
    token_mask,
    first_gate,
    first_up,
    first_down,
    bias_weight,
    query_weight,
    key_weight,
    value_weight,
    gate_weight,
    out_weight,
    second_gate,
    second_up,
    second_down,
):
    rows_here, keys_here, channels = pair_state.shape
    cols = lax.axis_size("col")
    own_count, width = single_state.shape
    core = lax.axis_index("col") % 2
    heads = bias_weight.shape[1]
    head_dim = width // heads
    widened = pair_state.astype(jnp.float32)
    updated = (widened + transition(widened, first_gate, first_up, first_down)).astype(jnp.bfloat16)
    flipped = mirror(updated)

    query_rows = spread_rows(single_state)
    key_rows = lax.ppermute(
        lax.dynamic_slice_in_dim(query_rows, core * keys_here, keys_here, 0), PAIR, mirror_pairs(0)
    )
    query_normed = norm_rows(query_rows.astype(jnp.float32)).astype(jnp.bfloat16)
    queries = jnp.dot(query_normed, query_weight, preferred_element_type=jnp.float32).astype(
        jnp.bfloat16
    )
    key_normed = norm_rows(key_rows.astype(jnp.float32)).astype(jnp.bfloat16)
    key_vecs = jnp.dot(key_normed, key_weight, preferred_element_type=jnp.float32).astype(
        jnp.bfloat16
    )
    value_vecs = jnp.dot(key_normed, value_weight, preferred_element_type=jnp.float32).astype(
        jnp.bfloat16
    )
    bias_normed = norm_rows(updated.astype(jnp.float32)).astype(jnp.bfloat16)
    pair_bias = jnp.einsum(
        "ijc,ch->hij", bias_normed, bias_weight, preferred_element_type=jnp.float32
    )
    scores = (
        jnp.einsum(
            "ihd,jhd->hij",
            queries.reshape(rows_here, heads, head_dim),
            key_vecs.reshape(keys_here, heads, head_dim),
            preferred_element_type=jnp.float32,
        )
        * (1.0 / math.sqrt(head_dim))
        + pair_bias
    )
    scores = jnp.where(token_mask[None, None, :] > 0, scores, -1000000000.0)
    top = jnp.max(scores, axis=2)
    weights = jnp.exp(scores - top[:, :, None])
    total = jnp.sum(weights, axis=2)
    value_heads = value_vecs.astype(jnp.float32).reshape(keys_here, heads, head_dim)
    sums = jnp.einsum("hij,jhd->ihd", weights, value_heads, precision=lax.Precision.HIGHEST)
    parts = jnp.concatenate(
        [
            sums.reshape(cols, own_count * width),
            jnp.transpose(top).reshape(cols, own_count * heads),
            jnp.transpose(total).reshape(cols, own_count * heads),
            jnp.zeros((cols, 2048 - own_count * (width + 2 * heads)), jnp.float32),
        ],
        axis=1,
    ).reshape(cols, 16, 128)
    got = lax.all_to_all(parts, "col", split_axis=0, concat_axis=0, tiled=True).reshape(cols, 2048)
    cut = own_count * width
    sums = got[:, :cut].reshape(cols, own_count, heads, head_dim)
    top = got[:, cut : cut + own_count * heads].reshape(cols, own_count, heads)
    total = got[:, cut + own_count * heads : cut + 2 * own_count * heads].reshape(
        cols, own_count, heads
    )
    scale = jnp.exp(top - jnp.max(top, axis=0, keepdims=True))
    numerator = jnp.sum(sums * scale[..., None], axis=0)
    denominator = jnp.sum(total * scale, axis=0)
    attended = (numerator / denominator[..., None]).reshape(own_count, width)
    own_normed = norm_rows(single_state.astype(jnp.float32)).astype(jnp.bfloat16)
    gate_act = jax.nn.sigmoid(jnp.dot(own_normed, gate_weight, preferred_element_type=jnp.float32))
    gated = (gate_act * attended).astype(jnp.bfloat16)
    own_out = (
        single_state.astype(jnp.float32)
        + jnp.dot(gated, out_weight, preferred_element_type=jnp.float32)
    ).astype(jnp.bfloat16)
    single_out = spread_rows(own_out)

    summed = updated.astype(jnp.float32) + flipped.astype(jnp.float32)
    pair_out = (summed + transition(summed, second_gate, second_up, second_down)).astype(
        jnp.bfloat16
    )
    return (pair_out, single_out)


def solution(mesh):
    in_specs = (P("row", "col", None), P(("row", "col"), None), P("col")) + (P(),) * 12
    out_specs = (P("row", "col", None), P("row", None))
    return jax.shard_map(body, mesh=mesh, in_specs=in_specs, out_specs=out_specs, check_vma=False)
```

```python
import math

import jax
import jax.numpy as jnp
import numpy as np
from jax import lax
from jax.experimental import pallas as pl
from jax.experimental.pallas import tpu as pltpu
from jax.sharding import PartitionSpec as P


PAIR = ("row", "col")
STEP = 16
CUT = 512
VMEM = 20 << 20
WIDE = 56 << 20


def norm_rows(values):
    centre = jnp.mean(values, axis=-1, keepdims=True)
    centred = values - centre
    spread = jnp.mean(centred * centred, axis=-1, keepdims=True)
    return centred * lax.rsqrt(spread + 1e-05)


def transition(cells, gate_ref, up_ref, down_ref):
    normed = norm_rows(cells).astype(jnp.bfloat16)
    total = cells
    for start in range(0, gate_ref.shape[1], CUT):
        cut = slice(start, start + CUT)
        half = 0.5 * jnp.dot(normed, gate_ref[:, cut], preferred_element_type=jnp.float32)
        up_act = jnp.dot(normed, up_ref[:, cut], preferred_element_type=jnp.float32)
        hidden = ((half + half * jnp.tanh(half)) * up_act).astype(jnp.bfloat16)
        total = total + jnp.dot(hidden, down_ref[cut], preferred_element_type=jnp.float32)
    return total


def first_kernel(_, pair_ref, gate_ref, up_ref, down_ref, bias_ref, out_ref, pair_bias_ref):
    rows, cols, channels = pair_ref.shape
    cells = pair_ref[...].reshape(rows * cols, channels).astype(jnp.float32)
    updated = transition(cells, gate_ref, up_ref, down_ref).astype(jnp.bfloat16)
    out_ref[...] = updated.reshape(rows, cols, channels)
    normed = norm_rows(updated.astype(jnp.float32)).astype(jnp.bfloat16)
    pair_bias_ref[...] = lax.dot_general(
        bias_ref[...], normed, (((1,), (1,)), ((), ())), preferred_element_type=jnp.float32
    )


def second_kernel(_, left_ref, mid_ref, right_ref, got_ref, swap_ref, gate_ref, up_ref, down_ref, *rest):
    out_ref = rest[-1]
    channels = got_ref.shape[-1]
    pieces = []
    for part, own_ref in enumerate((left_ref, mid_ref, right_ref)):
        cut = slice(part * STEP, (part + 1) * STEP)
        got = got_ref[cut].reshape(STEP * STEP, channels)
        flipped = jnp.dot(swap_ref[...], got, preferred_element_type=jnp.float32)
        pieces.append(own_ref[...].reshape(STEP * STEP, channels).astype(jnp.float32) + flipped)
    cells = jnp.concatenate(pieces, axis=0)
    out = transition(cells, gate_ref, up_ref, down_ref).astype(jnp.bfloat16)
    for part in range(len(pieces)):
        cut = slice(part * STEP, (part + 1) * STEP)
        piece = out[part * STEP * STEP : (part + 1) * STEP * STEP]
        out_ref[:, cut] = piece.reshape(STEP, STEP, channels)


def whole(array):
    zeros = (0,) * array.ndim
    return pl.BlockSpec(array.shape, lambda i, s: zeros)


def cost(cells, channels, hidden):
    return pl.CostEstimate(
        flops=6 * cells * channels * hidden,
        bytes_accessed=6 * cells * channels,
        transcendentals=cells * hidden,
    )


def first_pass(core, pair_state, flip, part, weights, bias_weight):
    rows, _, channels = pair_state.shape
    half, heads = rows // 2, bias_weight.shape[0]
    block = lambda i, s: ((s[0] + flip) % 2, part, 0)
    return pl.pallas_call(
        first_kernel,
        grid_spec=pltpu.PrefetchScalarGridSpec(
            num_scalar_prefetch=1,
            grid=(1,),
            in_specs=[pl.BlockSpec((half, STEP, channels), block)]
            + [whole(w) for w in (*weights, bias_weight)],
            out_specs=[
                pl.BlockSpec((half, STEP, channels), lambda i, s: (0, 0, 0)),
                pl.BlockSpec((heads, half * STEP), lambda i, s: (0, 0)),
            ],
        ),
        out_shape=[
            jax.ShapeDtypeStruct((half, STEP, channels), jnp.bfloat16),
            jax.ShapeDtypeStruct((heads, half * STEP), jnp.float32),
        ],
        cost_estimate=cost(half * STEP, channels, weights[0].shape[1]),
        compiler_params=pltpu.CompilerParams(vmem_limit_bytes=VMEM if part or flip else WIDE),
        name="first_pass",
    )(core, pair_state, *weights, bias_weight)


def second_pass(core, owns, got, flip, part, swap, weights, out, shape):
    half, channels = got.shape[0], got.shape[-1]
    per_half = half // STEP
    own = pl.BlockSpec((STEP, STEP, channels), lambda i, s: (part, 0, 0))
    in_specs = [own] * 3 + [whole(a) for a in (got, swap, *weights)]
    operands = [*owns, got, swap, *weights]
    aliases = {}
    if out is not None:
        aliases = {1 + len(operands): 0}
        operands.append(out)
        in_specs.append(pl.BlockSpec(memory_space=pl.ANY))
    return pl.pallas_call(
        second_kernel,
        grid_spec=pltpu.PrefetchScalarGridSpec(
            num_scalar_prefetch=1,
            grid=(1,),
            in_specs=in_specs,
            out_specs=pl.BlockSpec(
                (STEP, shape[1], channels),
                lambda i, s: ((s[0] + flip) % 2 * per_half + part, 0, 0),
            ),
        ),
        out_shape=jax.ShapeDtypeStruct(shape, jnp.bfloat16),
        input_output_aliases=aliases,
        cost_estimate=cost(half * STEP, channels, weights[0].shape[1]),
        compiler_params=pltpu.CompilerParams(vmem_limit_bytes=VMEM),
        name="second_pass",
    )(core, *operands)


def mirror_pairs(flip):
    rows, cols = lax.axis_size("row"), lax.axis_size("col")
    pairs = []
    for row in range(rows):
        for col in range(cols):
            core, chip = col % 2, col // 2
            pairs.append((row * cols + col, chip * cols + 2 * row + (core ^ flip)))
    return pairs


def spread_rows(rows):
    count, channels = rows.shape
    cols = lax.axis_size("col")
    folded = rows.reshape(count * channels // 128, 128)
    padded = jnp.pad(folded, ((0, 16 - folded.shape[0]), (0, 0)))
    copies = jnp.broadcast_to(padded[None], (cols, 16, 128))
    got = lax.all_to_all(copies, "col", split_axis=0, concat_axis=0, tiled=True)
    return got[:, : folded.shape[0]].reshape(cols * count, channels)


def turn_rows(rows, core):
    half = rows.shape[0] // 2
    return jnp.where(core == 0, rows, jnp.concatenate([rows[half:], rows[:half]], axis=0))


def local_attention(query_rows, key_rows, pair_bias, token_mask, w_query, w_key, w_value, heads):
    rows_here, width = query_rows.shape
    keys_here = key_rows.shape[0]
    head_dim = width // heads
    query_normed = norm_rows(query_rows.astype(jnp.float32)).astype(jnp.bfloat16)
    key_normed = norm_rows(key_rows.astype(jnp.float32)).astype(jnp.bfloat16)
    queries = jnp.dot(query_normed, w_query, preferred_element_type=jnp.float32)
    key_vecs = jnp.dot(key_normed, w_key, preferred_element_type=jnp.float32)
    value_vecs = jnp.dot(key_normed, w_value, preferred_element_type=jnp.float32)
    scores = (
        jnp.einsum(
            "ihd,jhd->hij",
            queries.astype(jnp.bfloat16).reshape(rows_here, heads, head_dim),
            key_vecs.astype(jnp.bfloat16).reshape(keys_here, heads, head_dim),
            preferred_element_type=jnp.float32,
        )
        * (1.0 / math.sqrt(head_dim))
        + pair_bias
    )
    scores = jnp.where(token_mask[None, None, :] > 0, scores, -1000000000.0)
    top = jnp.max(scores, axis=2)
    weights = jnp.exp(scores - top[:, :, None])
    total = jnp.sum(weights, axis=2)
    value_heads = value_vecs.astype(jnp.bfloat16).astype(jnp.float32)
    value_heads = value_heads.reshape(keys_here, heads, head_dim)
    sums = jnp.einsum("hij,jhd->ihd", weights, value_heads, precision=lax.Precision.HIGHEST)
    return jnp.transpose(top), jnp.transpose(total), sums.reshape(rows_here, width)


def combine(got, own_count, width, heads):
    cols = got.shape[0]
    head_dim = width // heads
    cut, few = own_count * width, own_count * heads
    sums = got[:, :cut].reshape(cols, own_count, heads, head_dim)
    top = got[:, cut : cut + few].reshape(cols, own_count, heads)
    total = got[:, cut + few : cut + 2 * few].reshape(cols, own_count, heads)
    scale = jnp.exp(top - jnp.max(top, axis=0, keepdims=True))
    numerator = jnp.sum(sums * scale[..., None], axis=0)
    denominator = jnp.sum(total * scale, axis=0)
    return (numerator / denominator[..., None]).reshape(own_count, width)


def body(
    pair_state,
    single_state,
    token_mask,
    first_gate,
    first_up,
    first_down,
    bias_weight,
    query_weight,
    key_weight,
    value_weight,
    gate_weight,
    out_weight,
    second_gate,
    second_up,
    second_down,
):
    rows_here, keys_here, _ = pair_state.shape
    cols = lax.axis_size("col")
    own_count, width = single_state.shape
    core = lax.axis_index("col") % 2
    which = core.astype(jnp.int32).reshape(1)
    heads = bias_weight.shape[1]
    parts = keys_here // STEP
    first_weights = (first_gate, first_up, first_down)
    second_weights = (second_gate, second_up, second_down)

    query_rows = spread_rows(single_state)
    bias_heads = jnp.transpose(bias_weight)
    updated, bias, arrived = {}, {}, {}
    for part in range(parts):
        for flip in (0, 1):
            updated[flip, part], bias[flip, part] = first_pass(
                which, pair_state, flip, part, first_weights, bias_heads
            )
            arrived[flip, part] = lax.ppermute(updated[flip, part], PAIR, mirror_pairs(flip))

    key_rows = lax.ppermute(
        lax.dynamic_slice_in_dim(query_rows, core * keys_here, keys_here, 0),
        PAIR,
        mirror_pairs(0),
    )
    key_rows, bias = lax.optimization_barrier((key_rows, bias))
    half = rows_here // 2
    pair_bias = jnp.concatenate(
        [
            jnp.concatenate(
                [bias[flip, part].reshape(heads, half, STEP) for part in range(parts)], axis=2
            )
            for flip in (0, 1)
        ],
        axis=1,
    )
    top, total, sums = local_attention(
        turn_rows(query_rows, core),
        key_rows,
        pair_bias,
        token_mask,
        query_weight,
        key_weight,
        value_weight,
        heads,
    )
    state = turn_rows(jnp.concatenate([sums, top, total], axis=1), core)
    cut = own_count * width
    few = own_count * heads
    packed = jnp.concatenate(
        [
            state[:, :width].reshape(cols, cut),
            state[:, width : width + heads].reshape(cols, few),
            state[:, width + heads :].reshape(cols, few),
            jnp.zeros((cols, 2048 - cut - 2 * few), jnp.float32),
        ],
        axis=1,
    ).reshape(cols, 16, 128)
    got = lax.all_to_all(packed, "col", split_axis=0, concat_axis=0, tiled=True)
    attended = combine(got.reshape(cols, 2048), own_count, width, heads)
    own_normed = norm_rows(single_state.astype(jnp.float32)).astype(jnp.bfloat16)
    gate_act = jax.nn.sigmoid(jnp.dot(own_normed, gate_weight, preferred_element_type=jnp.float32))
    gated = (gate_act * attended).astype(jnp.bfloat16)
    own_out = (
        single_state.astype(jnp.float32)
        + jnp.dot(gated, out_weight, preferred_element_type=jnp.float32)
    ).astype(jnp.bfloat16)
    single_out = spread_rows(own_out)

    cell = np.arange(STEP * STEP)
    swap = jnp.asarray(
        cell[:, None] // STEP + cell[:, None] % STEP * STEP == cell[None, :], jnp.bfloat16
    )
    pair_out = None
    for part in range(parts):
        for flip in (0, 1):
            pair_out = second_pass(
                which,
                [updated[flip, p] for p in range(parts)],
                arrived[flip, part],
                flip,
                part,
                swap,
                second_weights,
                pair_out,
                pair_state.shape,
            )
    return (pair_out, single_out)


def solution(mesh):
    in_specs = (P("row", "col", None), P(("row", "col"), None), P("col")) + (P(),) * 12
    out_specs = (P("row", "col", None), P("row", None))
    return jax.shard_map(body, mesh=mesh, in_specs=in_specs, out_specs=out_specs, check_vma=False)
```
